256 devices in a mesh: gx: 8 (over z), gy: 4 (over x), gz: 8 (over y, core).
Axes of the slice: x: 4, y: 4, z: 8, core: 2. Of those that a mesh axis runs over, the one named last changes fastest.
Arguments:
- field: float32 [1024, 1024, 512], P('gz', 'gx', 'gy'), may hold values from -6 to 6
- peaks: float32 [4], replicated, may hold values from -1.5 to 1.5
- tint: float32 [3], replicated, may hold values from -2 to 2
- light: float32 [3], replicated, may hold values from -1 to 1
Outputs:
- image: float32 [4, 1024, 512], P(None, ('gx', 'gz'), 'gy')
The draws below stay inside these ranges and needn't reach their ends.
All inputs are finite; a program needn't handle non-finite values.
Results may differ from the reference program's by a relative error of at most 0.0003.
Values sent between devices are 32-bit elements; how exact they have to be, the bound alone decides.
A program may use at most 256 MiB of HBM per device.

```python
import jax
import jax.numpy as jnp
from jax import lax

BUMPS = 4
NX = 1024
NY = 512
NZ = 1024


def shard_levels(own_key, dims, pieces, least, largest):
    def one(axis_at, blocks):
        draws = jax.random.uniform(jax.random.fold_in(jax.random.fold_in(own_key, 6), axis_at), (blocks,), jnp.float32, least / len(pieces), largest / len(pieces))
        return jnp.repeat(jnp.exp(draws), dims[axis_at] // blocks).reshape((-1,) + (1,) * (len(dims) - axis_at - 1))

    level = one(*pieces[0])
    for cut in pieces[1:]:
        level = level * one(*cut)
    return level


def bell_draw(rng, dims, deviation, limit, pieces=(), held_as=jnp.bfloat16):
    entries = jax.random.normal(rng, dims, jnp.float32) * deviation
    if len(pieces) > 0:
        entries = shard_levels(rng, dims, pieces, -0.22, 0.18) * entries
    return jnp.clip(entries, min=-limit, max=limit).astype(held_as)


def setup_inputs(seed: int = 0) -> dict:
    seeds = jax.random.split(jax.random.key(seed), 5)
    field = bell_draw(seeds[0], (NZ, NX, NY), 1.0, 6.0, ((0, 8), (1, 8), (2, 4)), jnp.float32)
    peaks = jnp.clip(jax.random.uniform(seeds[1], (BUMPS,), jnp.float32, -1.5, 1.5), -1.5, 1.5)
    tint = jnp.clip(jax.random.uniform(seeds[2], (3,), jnp.float32, -2.0, 2.0), -2.0, 2.0)
    light = jnp.clip(jax.random.uniform(seeds[3], (3,), jnp.float32, -1.0, 1.0), -1.0, 1.0)
    return dict(field=field, peaks=peaks, tint=tint, light=light)


extinction = 1.5

def shading(center, grad_x, grad_y, grad_z, peaks, tint, light, depth):
    bump = jnp.zeros_like(center)
    for index in range(peaks.shape[0]):
        bump = bump + jnp.exp(-2.0 * (center - peaks[index]) ** 2)
    tau = extinction / depth * bump
    inverse = lax.rsqrt(grad_x * grad_x + grad_y * grad_y + grad_z * grad_z + 1.0)
    shade = 0.3 + 0.7 * jnp.abs(grad_x * light[0] + grad_y * light[1] + grad_z * light[2]) * inverse
    colour = jnp.stack([jax.nn.sigmoid(tint[c] * center) * shade for c in range(3)])
    return (tau, colour)

def rolled_grad(center, axis):
    return (8.0 * (jnp.roll(center, -1, axis) - jnp.roll(center, 1, axis)) - (jnp.roll(center, -2, axis) - jnp.roll(center, 2, axis))) / 12.0

def reference(field, peaks, tint, light):
    if NX % 64 == 0:
        step_rows = 64
    else:
        step_rows = NX

    def one_block(block):
        rows = (block * step_rows + jnp.arange(step_rows + 4, dtype=jnp.int32) - 2) % NX
        slab = jnp.take(field, rows.astype(jnp.int32), axis=1)
        center = slab[:, 2:-2]
        grad_x = (8.0 * (slab[:, 3:-1] - slab[:, 1:-3]) - (slab[:, 4:] - slab[:, :-4])) / 12.0
        grad_y = rolled_grad(center, 2)
        grad_z = rolled_grad(center, 0)
        tau, colour = shading(center, grad_x, grad_y, grad_z, peaks, tint, light, NZ)
        optical = jnp.cumsum(tau, axis=0)
        weight = jnp.exp(tau - optical) * (1.0 - jnp.exp(-tau))
        colours = lax.optimization_barrier(jnp.sum(weight[None] * colour, axis=1))
        alpha = 1.0 - jnp.exp(-optical[-1])
        return jnp.concatenate([colours, alpha[None]], axis=0)
    blocks = lax.map(one_block, jnp.arange(NX // step_rows, dtype=jnp.int32))
    return jnp.transpose(blocks, (1, 0, 2, 3)).reshape(4, NX, NY)
```

```python
import functools
import math

import jax
import jax.numpy as jnp
from jax import lax
from jax.experimental import pallas as pl
from jax.experimental.pallas import tpu as pltpu
from jax.sharding import PartitionSpec as P

extinction = 1.5
LOG2E = math.log2(math.e)
MESH = pl.DeviceIdType.MESH
ROWS = 16
GROUP = 32
UNROLL = 32


def kernel(
    nx, ny, nz, depth, field, peaks, tint, light, out,
    cells, eighth, border, to_right, to_left, from_left, from_right, piece, pieces,
    load_sem, x_send, x_recv, z_send, z_recv, y_send, y_recv, p_send, p_recv,
):
    zs, xs, lanes = field.shape
    groups = zs // GROUP
    blocks = xs // ROWS
    mx, my, mz = lax.axis_index("gx"), lax.axis_index("gy"), lax.axis_index("gz")
    left_x, right_x = lax.rem(mx + nx - 1, nx), lax.rem(mx + 1, nx)
    left_y, right_y = lax.rem(my + ny - 1, ny), lax.rem(my + 1, ny)
    left_z, right_z = lax.rem(mz + nz - 1, nz), lax.rem(mz + 1, nz)

    def block_of(step):
        return lax.rem(mz + 1 + step, nz)

    def rows_of(step):
        return pl.multiple_of(block_of(step) * ROWS, ROWS)

    def load(step):
        return pltpu.make_async_copy(
            field.at[:, pl.ds(rows_of(step), ROWS), :],
            cells.at[2 : zs + 2, pl.ds(rows_of(step) + 8, ROWS), :],
            load_sem.at[step],
        )

    for step in range(blocks):
        load(step).start()

    barrier = pltpu.get_barrier_semaphore()
    greeted = 0
    for name, who in (("gx", left_x), ("gx", right_x), ("gy", left_y), ("gy", right_y)):
        pl.semaphore_signal(barrier, inc=1, device_id={name: who}, device_id_type=MESH)
        greeted += 1
    for k in range(1, nz):
        pl.semaphore_signal(
            barrier, inc=1, device_id={"gz": lax.rem(mz + k, nz)}, device_id_type=MESH
        )
        greeted += 1

    lane = lax.broadcasted_iota(jnp.int32, (ROWS, lanes), 1)
    lane_group = lane >> 2
    lane_column = lane & 3
    first_pair = lane_column < 2

    def pack(step):
        rows = rows_of(step)

        packed = [jnp.zeros((ROWS, lanes), jnp.float32)] * groups
        for z in range(GROUP):
            here = lane_group == z
            for g in range(groups):
                v = cells[2 + g * GROUP + z, pl.ds(rows + 8, ROWS), :]
                eighth[2 + g * GROUP + z, pl.ds(rows + 8, ROWS), :] = 0.125 * v
                packed[g] = jnp.where(here, pltpu.roll(v, (4 * z + 2) % lanes, 1), packed[g])
        for g in range(groups):
            border[g, pl.ds(rows, ROWS), :] = packed[g]
        for g in range(0, groups, 2):
            even, odd = packed[g], packed[g + 1]
            to_right[step, g // 2] = jnp.where(first_pair, even, pltpu.roll(odd, 2, 1))
            to_left[step, g // 2] = jnp.where(first_pair, pltpu.roll(odd, lanes - 2, 1), even)

    def y_copies(step):
        right = pltpu.make_async_remote_copy(
            to_right.at[step], from_left.at[step], y_send.at[0, step], y_recv.at[0, step],
            device_id={"gy": right_y}, device_id_type=MESH,
        )
        left = pltpu.make_async_remote_copy(
            to_left.at[step], from_right.at[step], y_send.at[1, step], y_recv.at[1, step],
            device_id={"gy": left_y}, device_id_type=MESH,
        )
        return right, left

    inner = pl.ds(8, xs)
    halos = [
        pltpu.make_async_remote_copy(
            field.at[zs - 2 : zs], cells.at[0:2, inner, :], z_send.at[0], z_recv.at[0],
            device_id={"gz": right_z}, device_id_type=MESH,
        ),
        pltpu.make_async_remote_copy(
            field.at[0:2], cells.at[zs + 2 : zs + 4, inner, :], z_send.at[1], z_recv.at[1],
            device_id={"gz": left_z}, device_id_type=MESH,
        ),
        pltpu.make_async_remote_copy(
            field.at[:, xs - 2 : xs, :], cells.at[2 : zs + 2, 6:8, :], x_send.at[0], x_recv.at[0],
            device_id={"gx": right_x}, device_id_type=MESH,
        ),
        pltpu.make_async_remote_copy(
            field.at[:, 0:2, :], cells.at[2 : zs + 2, xs + 8 : xs + 10, :], x_send.at[1],
            x_recv.at[1], device_id={"gx": left_x}, device_id_type=MESH,
        ),
    ]

    load(0).wait()
    pack(0)
    pl.semaphore_wait(barrier, greeted)
    for copy in halos:
        copy.start()
    for copy in y_copies(0):
        copy.start()

    @pl.loop(1, blocks)
    def _(step):
        load(step).wait()
        pack(step)
        for copy in y_copies(step):
            copy.start()

    def correction(step):
        rows = rows_of(step)
        for g in range(0, groups, 2):
            left, right = from_left[step, g // 2], from_right[step, g // 2]
            for odd in range(2):
                if odd:
                    outer = jnp.where(
                        first_pair, pltpu.roll(left, lanes - 2, 1), pltpu.roll(right, 2, 1)
                    )
                else:
                    outer = jnp.where(first_pair, left, right)
                diff = outer - border[g + odd, pl.ds(rows, ROWS), :]
                p2, p1 = pltpu.roll(diff, lanes - 2, 1), pltpu.roll(diff, lanes - 1, 1)
                m2, m1 = pltpu.roll(diff, 2, 1), pltpu.roll(diff, 1, 1)
                far = 0.125 * jnp.where(first_pair, -p2, m2)
                near = jnp.where(lane_column == 1, p1, jnp.where(lane_column == 2, -m1, 0.0))
                border[g + odd, pl.ds(rows, ROWS), :] = near + far

    unit = extinction / depth * LOG2E
    first = peaks[0]
    slopes = [4.0 * LOG2E * (peaks[i] - first) for i in range(1, peaks.shape[0])]
    offsets = [
        math.log2(unit) - 2.0 * LOG2E * (peaks[i] * peaks[i] - first * first)
        for i in range(1, peaks.shape[0])
    ]
    tints = [0.5 * tint[c] for c in range(3)]
    lights = [0.7 * light[c] for c in range(3)]
    edge = (lane < 2) | (lane >= lanes - 2)

    def march(step):
        rows = rows_of(step)
        base = rows + 8
        mid = pl.ds(base, ROWS)

        def one_group(g, carry):
            fix_all = border[g, pl.ds(rows, ROWS), :]

            def some(i, carry):
                total, trans, s0, s1, s2, s3 = carry
                for j in range(UNROLL):
                    zl = i * UNROLL + j
                    z = g * GROUP + zl + 2
                    f, f8 = cells[z, mid, :], eighth[z, mid, :]
                    gz = (cells[z + 1, mid, :] - cells[z - 1, mid, :]) - (
                        eighth[z + 2, mid, :] - eighth[z - 2, mid, :]
                    )
                    gx = (
                        cells[z, pl.ds(base + 1, ROWS), :] - cells[z, pl.ds(base - 1, ROWS), :]
                    ) - (eighth[z, pl.ds(base + 2, ROWS), :] - eighth[z, pl.ds(base - 2, ROWS), :])
                    gy = (pltpu.roll(f, lanes - 1, 1) - pltpu.roll(f, 1, 1)) - (
                        pltpu.roll(f8, lanes - 2, 1) - pltpu.roll(f8, 2, 1)
                    )
                    fix = pltpu.roll(fix_all, (2 * lanes - 2 - 4 * zl) % lanes, 1)
                    gy = jnp.where(edge, gy + fix, gy)
                    inverse = lax.rsqrt((gx * gx + gy * gy) + (gz * gz + 2.25))
                    lit = jnp.abs(gx * lights[0] + gy * lights[1] + gz * lights[2])
                    bumps = unit
                    for k in range(len(slopes)):
                        bumps = bumps + jnp.exp2(f * slopes[k] + offsets[k])
                    away = f - first
                    total = total - jnp.exp2(away * away * (-2.0 * LOG2E)) * bumps
                    after = jnp.exp2(total)
                    shaded = (trans - after) * (0.3 + lit * inverse)
                    trans = after
                    s0 = s0 + shaded
                    s1 = s1 + shaded * jnp.tanh(f * tints[0])
                    s2 = s2 + shaded * jnp.tanh(f * tints[1])
                    s3 = s3 + shaded * jnp.tanh(f * tints[2])
                return total, trans, s0, s1, s2, s3

            if UNROLL == GROUP:
                return some(0, carry)
            return lax.fori_loop(0, GROUP // UNROLL, some, carry)

        zero = jnp.zeros((ROWS, lanes), jnp.float32)
        start = (zero, zero + 1.0, zero, zero, zero, zero)
        total, _, s0, s1, s2, s3 = lax.fori_loop(0, groups, one_group, start)
        return 0.5 * (s0 + s1), 0.5 * (s0 + s2), 0.5 * (s0 + s3), total

    def p_copy(step):
        return pltpu.make_async_remote_copy(
            piece.at[step], pieces.at[mz], p_send.at[step], p_recv.at[mz],
            device_id={"gz": block_of(step)}, device_id_type=MESH,
        )

    for copy in halos:
        copy.wait_recv()
    for z in (0, 1, zs + 2, zs + 3):
        eighth[z, inner, :] = 0.125 * cells[z, inner, :]

    @pl.loop(0, zs // 8)
    def _(i):
        for rows in (pl.ds(6, 2), pl.ds(xs + 8, 2)):
            eighth[pl.ds(i * 8 + 2, 8), rows, :] = 0.125 * cells[pl.ds(i * 8 + 2, 8), rows, :]

    @pl.loop(0, blocks)
    def _(step):
        for copy in y_copies(step):
            copy.wait_recv()
        correction(step)
        results = march(step)

        @pl.when(step < blocks - 1)
        def _():
            for c in range(4):
                piece[step, c] = results[c]
            p_copy(step).start()

        @pl.when(step == blocks - 1)
        def _():
            for c in range(4):
                pieces[mz, c] = results[c]

    for k in range(1, nz):
        source = lax.rem(mz + k, nz)
        pltpu.make_async_remote_copy(
            piece.at[0], pieces.at[source], p_send.at[0], p_recv.at[source],
            device_id={"gz": source}, device_id_type=MESH,
        ).wait_recv()

    before = None
    for k in range(nz):
        if k == 0:
            image = [pieces[0, c] for c in range(3)]
            optical = pieces[0, 3]
        else:
            before = jnp.exp2(optical)
            image = [image[c] + before * pieces[k, c] for c in range(3)]
            optical = optical + pieces[k, 3]
    for c in range(3):
        out[c] = image[c]
    out[3] = 1.0 - jnp.exp2(optical)

    for copy in halos:
        copy.wait_send()
    for step in range(blocks):
        for copy in y_copies(step):
            copy.wait_send()
    for step in range(blocks - 1):
        p_copy(step).wait_send()


def render(sizes, field, peaks, tint, light):
    nx, ny, nz = sizes
    zs, xs, lanes = field.shape
    groups, blocks = zs // GROUP, xs // ROWS
    f32 = jnp.float32
    packed = pltpu.VMEM((blocks, groups // 2, ROWS, lanes), f32)
    dma = pltpu.SemaphoreType.DMA
    smem = pl.BlockSpec(memory_space=pltpu.SMEM)
    return pl.pallas_call(
        functools.partial(kernel, nx, ny, nz, zs * nz),
        out_shape=jax.ShapeDtypeStruct((4, ROWS, lanes), f32),
        in_specs=[pl.BlockSpec(memory_space=pl.ANY), smem, smem, smem],
        out_specs=pl.BlockSpec(memory_space=pltpu.VMEM),
        scratch_shapes=[
            pltpu.VMEM((zs + 4, xs + 16, lanes), f32),
            pltpu.VMEM((zs + 4, xs + 16, lanes), f32),
            pltpu.VMEM((groups, xs, lanes), f32),
            packed, packed, packed, packed,
            pltpu.VMEM((blocks, 4, ROWS, lanes), f32),
            pltpu.VMEM((nz, 4, ROWS, lanes), f32),
            dma((blocks,)), dma((2,)), dma((2,)), dma((2,)), dma((2,)),
            dma((2, blocks)), dma((2, blocks)), dma((blocks,)), dma((nz,)),
        ],
        compiler_params=pltpu.CompilerParams(collective_id=0, has_side_effects=True),
    )(field, peaks, tint, light)


def solution(mesh):
    sizes = (mesh.shape["gx"], mesh.shape["gy"], mesh.shape["gz"])
    in_specs = (P("gz", "gx", "gy"), P(), P(), P())
    out_specs = P(None, ("gx", "gz"), "gy")
    return jax.shard_map(
        functools.partial(render, sizes),
        mesh=mesh, in_specs=in_specs, out_specs=out_specs, check_vma=False,
    )
```

```python
import functools
import math

import jax
import jax.numpy as jnp
from jax import lax
from jax.experimental import pallas as pl
from jax.experimental.pallas import tpu as pltpu
from jax.sharding import PartitionSpec as P

extinction = 1.5
LOG2E = math.log2(math.e)
MESH = pl.DeviceIdType.MESH
ROWS = 16
GROUP = 32
UNROLL = 32
SEND_X = 1


def kernel(
    nx, ny, nz, depth, field, peaks, tint, light, out,
    cells, eighth, border, to_right, to_left, from_left, from_right, piece, pieces,
    load_sem, x_send, x_recv, z_send, z_recv, y_send, y_recv, p_send, p_recv, entered,
):
    zs, xs, lanes = field.shape
    groups = zs // GROUP
    blocks = xs // ROWS
    mx, my, mz = lax.axis_index("gx"), lax.axis_index("gy"), lax.axis_index("gz")
    left_x, right_x = lax.rem(mx + nx - 1, nx), lax.rem(mx + 1, nx)
    left_y, right_y = lax.rem(my + ny - 1, ny), lax.rem(my + 1, ny)
    left_z, right_z = lax.rem(mz + nz - 1, nz), lax.rem(mz + 1, nz)

    bordering = 1 - (lax.rem(mz, nz - 1) + nz - 2) // (nz - 1)
    parity = lax.rem(mz, 2)

    def block_of(step):
        from_0, from_1, from_2 = ((step + k) // nz for k in (3, 2, 1))
        inside = lax.rem(mz + step, nz - 2) + 1
        border_one = bordering * inside + (1 - bordering) * parity * (nz - 1)
        border_two = bordering * (nz - 1 - mz) + (1 - bordering) * (1 - parity) * (nz - 1)
        return (
            (1 - from_0) * inside
            + (from_0 - from_1) * border_one
            + (from_1 - from_2) * border_two
            + from_2 * mz
        )

    def rows_of(step):
        return pl.multiple_of(block_of(step) * ROWS, ROWS)

    def load(step):
        return pltpu.make_async_copy(
            field.at[:, pl.ds(rows_of(step), ROWS), :],
            cells.at[2 : zs + 2, pl.ds(rows_of(step) + 8, ROWS), :],
            load_sem.at[step],
        )

    for step in range(blocks):
        load(step).start()

    barrier = pltpu.get_barrier_semaphore()
    above_first, at_last = (mx + nx - 1) // nx, (mx + 1) // nx

    @pl.when(mx < nx - 1)
    def _():
        pl.semaphore_signal(barrier, inc=1, device_id={"gx": right_x}, device_id_type=MESH)

    @pl.when(mx == 0)
    def _():
        pl.semaphore_signal(barrier, inc=1, device_id={"gx": left_x}, device_id_type=MESH)

    for who in (left_y, right_y):
        pl.semaphore_signal(barrier, inc=1, device_id={"gy": who}, device_id_type=MESH)
    for k in range(1, nz):
        pl.semaphore_signal(
            barrier, inc=1, device_id={"gz": lax.rem(mz + k, nz)}, device_id_type=MESH
        )
    greeted = nz + 1 + above_first + at_last

    lane = lax.broadcasted_iota(jnp.int32, (ROWS, lanes), 1)
    lane_group = lane >> 2
    lane_column = lane & 3
    first_pair = lane_column < 2

    def pack(step):
        rows = rows_of(step)

        packed = [jnp.zeros((ROWS, lanes), jnp.float32)] * groups
        for z in range(GROUP):
            here = lane_group == z
            for g in range(groups):
                v = cells[2 + g * GROUP + z, pl.ds(rows + 8, ROWS), :]
                eighth[2 + g * GROUP + z, pl.ds(rows + 8, ROWS), :] = 0.125 * v
                packed[g] = jnp.where(here, pltpu.roll(v, (4 * z + 2) % lanes, 1), packed[g])
        for g in range(groups):
            border[g, pl.ds(rows, ROWS), :] = packed[g]
        for g in range(0, groups, 2):
            even, odd = packed[g], packed[g + 1]
            to_right[step, g // 2] = jnp.where(first_pair, even, pltpu.roll(odd, 2, 1))
            to_left[step, g // 2] = jnp.where(first_pair, pltpu.roll(odd, lanes - 2, 1), even)

    def y_copies(step):
        right = pltpu.make_async_remote_copy(
            to_right.at[step], from_left.at[step], y_send.at[0, step], y_recv.at[0, step],
            device_id={"gy": right_y}, device_id_type=MESH,
        )
        left = pltpu.make_async_remote_copy(
            to_left.at[step], from_right.at[step], y_send.at[1, step], y_recv.at[1, step],
            device_id={"gy": left_y}, device_id_type=MESH,
        )
        return right, left

    inner = pl.ds(8, xs)
    z_copies = [
        pltpu.make_async_remote_copy(
            field.at[zs - 2 : zs], cells.at[0:2, inner, :], z_send.at[0], z_recv.at[0],
            device_id={"gz": right_z}, device_id_type=MESH,
        ),
        pltpu.make_async_remote_copy(
            field.at[0:2], cells.at[zs + 2 : zs + 4, inner, :], z_send.at[1], z_recv.at[1],
            device_id={"gz": left_z}, device_id_type=MESH,
        ),
    ]
    x_right = pltpu.make_async_remote_copy(
        field.at[:, xs - 2 : xs, :], cells.at[2 : zs + 2, 6:8, :], x_send.at[0], x_recv.at[0],
        device_id={"gx": right_x}, device_id_type=MESH,
    )
    x_left = pltpu.make_async_remote_copy(
        field.at[:, 0:2, :], cells.at[2 : zs + 2, xs + 8 : xs + 10, :], x_send.at[1],
        x_recv.at[1], device_id={"gx": left_x}, device_id_type=MESH,
    )

    load(0).wait()
    pack(0)
    pl.semaphore_wait(barrier, greeted)
    for copy in z_copies:
        copy.start()
    for copy in y_copies(0):
        copy.start()

    @pl.when(mx > 0)
    def _():
        pl.semaphore_signal(entered.at[1], inc=1, device_id={"gx": left_x}, device_id_type=MESH)
        x_left.start()

    @pl.when(mx == nx - 1)
    def _():
        pl.semaphore_signal(entered.at[0], inc=1, device_id={"gx": right_x}, device_id_type=MESH)
        x_right.start()

    @pl.loop(1, blocks)
    def _(step):
        load(step).wait()
        pack(step)
        for copy in y_copies(step):
            copy.start()

    def correction(step):
        rows = rows_of(step)
        for g in range(0, groups, 2):
            left, right = from_left[step, g // 2], from_right[step, g // 2]
            for odd in range(2):
                if odd:
                    outer = jnp.where(
                        first_pair, pltpu.roll(left, lanes - 2, 1), pltpu.roll(right, 2, 1)
                    )
                else:
                    outer = jnp.where(first_pair, left, right)
                diff = outer - border[g + odd, pl.ds(rows, ROWS), :]
                p2, p1 = pltpu.roll(diff, lanes - 2, 1), pltpu.roll(diff, lanes - 1, 1)
                m2, m1 = pltpu.roll(diff, 2, 1), pltpu.roll(diff, 1, 1)
                far = 0.125 * jnp.where(first_pair, -p2, m2)
                near = jnp.where(lane_column == 1, p1, jnp.where(lane_column == 2, -m1, 0.0))
                border[g + odd, pl.ds(rows, ROWS), :] = near + far

    unit = extinction / depth * LOG2E
    first = peaks[0]
    slopes = [4.0 * LOG2E * (peaks[i] - first) for i in range(1, peaks.shape[0])]
    offsets = [
        math.log2(unit) - 2.0 * LOG2E * (peaks[i] * peaks[i] - first * first)
        for i in range(1, peaks.shape[0])
    ]
    tints = [0.5 * tint[c] for c in range(3)]
    lights = [0.7 * light[c] for c in range(3)]
    edge = (lane < 2) | (lane >= lanes - 2)

    def march(step):
        rows = rows_of(step)
        base = rows + 8
        mid = pl.ds(base, ROWS)

        def one_group(g, carry):
            fix_all = border[g, pl.ds(rows, ROWS), :]

            def some(i, carry):
                total, trans, s0, s1, s2, s3 = carry
                for j in range(UNROLL):
                    zl = i * UNROLL + j
                    z = g * GROUP + zl + 2
                    f, f8 = cells[z, mid, :], eighth[z, mid, :]
                    gz = (cells[z + 1, mid, :] - cells[z - 1, mid, :]) - (
                        eighth[z + 2, mid, :] - eighth[z - 2, mid, :]
                    )
                    gx = (
                        cells[z, pl.ds(base + 1, ROWS), :] - cells[z, pl.ds(base - 1, ROWS), :]
                    ) - (eighth[z, pl.ds(base + 2, ROWS), :] - eighth[z, pl.ds(base - 2, ROWS), :])
                    gy = (pltpu.roll(f, lanes - 1, 1) - pltpu.roll(f, 1, 1)) - (
                        pltpu.roll(f8, lanes - 2, 1) - pltpu.roll(f8, 2, 1)
                    )
                    fix = pltpu.roll(fix_all, (2 * lanes - 2 - 4 * zl) % lanes, 1)
                    gy = jnp.where(edge, gy + fix, gy)
                    inverse = lax.rsqrt((gx * gx + gy * gy) + (gz * gz + 2.25))
                    lit = jnp.abs(gx * lights[0] + gy * lights[1] + gz * lights[2])
                    bumps = unit
                    for k in range(len(slopes)):
                        bumps = bumps + jnp.exp2(f * slopes[k] + offsets[k])
                    away = f - first
                    total = total - jnp.exp2(away * away * (-2.0 * LOG2E)) * bumps
                    after = jnp.exp2(total)
                    shaded = (trans - after) * (0.3 + lit * inverse)
                    trans = after
                    s0 = s0 + shaded
                    s1 = s1 + shaded * jnp.tanh(f * tints[0])
                    s2 = s2 + shaded * jnp.tanh(f * tints[1])
                    s3 = s3 + shaded * jnp.tanh(f * tints[2])
                return total, trans, s0, s1, s2, s3

            if UNROLL == GROUP:
                return some(0, carry)
            return lax.fori_loop(0, GROUP // UNROLL, some, carry)

        zero = jnp.zeros((ROWS, lanes), jnp.float32)
        start = (zero, zero + 1.0, zero, zero, zero, zero)
        total, _, s0, s1, s2, s3 = lax.fori_loop(0, groups, one_group, start)
        return 0.5 * (s0 + s1), 0.5 * (s0 + s2), 0.5 * (s0 + s3), total

    def p_copy(step):
        return pltpu.make_async_remote_copy(
            piece.at[step], pieces.at[mz], p_send.at[step], p_recv.at[mz],
            device_id={"gz": block_of(step)}, device_id_type=MESH,
        )

    for copy in z_copies:
        copy.wait_recv()
    for z in (0, 1, zs + 2, zs + 3):
        eighth[z, inner, :] = 0.125 * cells[z, inner, :]

    @pl.loop(0, blocks)
    def _(step):
        @pl.when(step == SEND_X)
        def _():
            @pl.when(mx == 0)
            def _():
                pl.semaphore_wait(entered.at[0], 1)
                x_left.start()

            @pl.when(mx < nx - 1)
            def _():
                pl.semaphore_wait(entered.at[1], 1)
                x_right.start()

        @pl.when(step == blocks - 3)
        def _():
            x_left.wait_recv()
            x_right.wait_recv()

            @pl.loop(0, zs // 8)
            def _(i):
                for rows in (pl.ds(6, 2), pl.ds(xs + 8, 2)):
                    z8 = pl.ds(i * 8 + 2, 8)
                    eighth[z8, rows, :] = 0.125 * cells[z8, rows, :]

        for copy in y_copies(step):
            copy.wait_recv()
        correction(step)
        results = march(step)

        @pl.when(step < blocks - 1)
        def _():
            for c in range(4):
                piece[step, c] = results[c]
            p_copy(step).start()

        @pl.when(step == blocks - 1)
        def _():
            for c in range(4):
                pieces[mz, c] = results[c]

    for k in range(1, nz):
        source = lax.rem(mz + k, nz)
        pltpu.make_async_remote_copy(
            piece.at[0], pieces.at[source], p_send.at[0], p_recv.at[source],
            device_id={"gz": source}, device_id_type=MESH,
        ).wait_recv()

    before = None
    for k in range(nz):
        if k == 0:
            image = [pieces[0, c] for c in range(3)]
            optical = pieces[0, 3]
        else:
            before = jnp.exp2(optical)
            image = [image[c] + before * pieces[k, c] for c in range(3)]
            optical = optical + pieces[k, 3]
    for c in range(3):
        out[c] = image[c]
    out[3] = 1.0 - jnp.exp2(optical)

    for copy in (x_left, x_right, *z_copies):
        copy.wait_send()
    for step in range(blocks):
        for copy in y_copies(step):
            copy.wait_send()
    for step in range(blocks - 1):
        p_copy(step).wait_send()


def render(sizes, field, peaks, tint, light):
    nx, ny, nz = sizes
    zs, xs, lanes = field.shape
    groups, blocks = zs // GROUP, xs // ROWS
    f32 = jnp.float32
    packed = pltpu.VMEM((blocks, groups // 2, ROWS, lanes), f32)
    dma = pltpu.SemaphoreType.DMA
    smem = pl.BlockSpec(memory_space=pltpu.SMEM)
    return pl.pallas_call(
        functools.partial(kernel, nx, ny, nz, zs * nz),
        out_shape=jax.ShapeDtypeStruct((4, ROWS, lanes), f32),
        in_specs=[pl.BlockSpec(memory_space=pl.ANY), smem, smem, smem],
        out_specs=pl.BlockSpec(memory_space=pltpu.VMEM),
        scratch_shapes=[
            pltpu.VMEM((zs + 4, xs + 16, lanes), f32),
            pltpu.VMEM((zs + 4, xs + 16, lanes), f32),
            pltpu.VMEM((groups, xs, lanes), f32),
            packed, packed, packed, packed,
            pltpu.VMEM((blocks, 4, ROWS, lanes), f32),
            pltpu.VMEM((nz, 4, ROWS, lanes), f32),
            dma((blocks,)), dma((2,)), dma((2,)), dma((2,)), dma((2,)),
            dma((2, blocks)), dma((2, blocks)), dma((blocks,)), dma((nz,)),
            pltpu.SemaphoreType.REGULAR((2,)),
        ],
        compiler_params=pltpu.CompilerParams(collective_id=0, has_side_effects=True),
    )(field, peaks, tint, light)


def solution(mesh):
    sizes = (mesh.shape["gx"], mesh.shape["gy"], mesh.shape["gz"])
    in_specs = (P("gz", "gx", "gy"), P(), P(), P())
    out_specs = P(None, ("gx", "gz"), "gy")
    return jax.shard_map(
        functools.partial(render, sizes),
        mesh=mesh, in_specs=in_specs, out_specs=out_specs, check_vma=False,
    )
```

```python
import functools
import math

import jax
import jax.numpy as jnp
from jax import lax
from jax.experimental import pallas as pl
from jax.experimental.pallas import tpu as pltpu
from jax.sharding import PartitionSpec as P

extinction = 1.5
LOG2E = math.log2(math.e)
MESH = pl.DeviceIdType.MESH
ROWS = 16
GROUP = 32
SEND_X = 0


def kernel(
    nx, ny, nz, depth, field, peaks, tint, light, out,
    cells, eighth, pair, pair_eighth, thick, border, to_right, to_left, from_left, from_right, piece, pieces,
    load_sem, x_send, x_recv, z_send, z_recv, y_send, y_recv, p_send, p_recv, entered,
):
    zs, xs, lanes = field.shape
    groups = zs // GROUP
    blocks = xs // ROWS
    mx, my, mz = lax.axis_index("gx"), lax.axis_index("gy"), lax.axis_index("gz")
    left_x, right_x = lax.rem(mx + nx - 1, nx), lax.rem(mx + 1, nx)
    left_y, right_y = lax.rem(my + ny - 1, ny), lax.rem(my + 1, ny)
    left_z, right_z = lax.rem(mz + nz - 1, nz), lax.rem(mz + 1, nz)

    above_zero, is_last = (mz + nz - 1) // nz, (mz + 1) // nz
    zero_step = max(1, nz - 4)

    def reached(step, bound):
        return (step + nz - bound) // nz

    def block_of(step):
        at_own = reached(step, nz - 1)
        at_zero = reached(step, zero_step) - reached(step, zero_step + 1)
        at_late = reached(step, nz - 2) - at_own
        place = step + 1 - above_zero * reached(step, zero_step + 1)
        inner_block = place + above_zero * reached(place, mz)
        late = is_last * inner_block + (1 - is_last) * (nz - 1)
        other = at_late * late + (1 - at_late) * inner_block
        return (1 - at_own) * (1 - at_zero * above_zero) * other + at_own * mz

    def rows_of(step):
        return pl.multiple_of(block_of(step) * ROWS, ROWS)

    def load(step):
        return pltpu.make_async_copy(
            field.at[:, pl.ds(rows_of(step), ROWS), :],
            cells.at[2 : zs + 2, pl.ds(rows_of(step) + 8, ROWS), :],
            load_sem.at[step],
        )

    for step in range(blocks):
        load(step).start()

    barrier = pltpu.get_barrier_semaphore()
    above_first, at_last = (mx + nx - 1) // nx, (mx + 1) // nx

    @pl.when(mx < nx - 1)
    def _():
        pl.semaphore_signal(barrier, inc=1, device_id={"gx": right_x}, device_id_type=MESH)

    @pl.when(mx == 0)
    def _():
        pl.semaphore_signal(barrier, inc=1, device_id={"gx": left_x}, device_id_type=MESH)

    for who in (left_y, right_y):
        pl.semaphore_signal(barrier, inc=1, device_id={"gy": who}, device_id_type=MESH)
    for k in range(1, nz):
        pl.semaphore_signal(
            barrier, inc=1, device_id={"gz": lax.rem(mz + k, nz)}, device_id_type=MESH
        )
    greeted = nz + 1 + above_first + at_last

    lane = lax.broadcasted_iota(jnp.int32, (ROWS, lanes), 1)
    lane_group = lane >> 2
    lane_column = lane & 3
    first_pair = lane_column < 2

    unit = extinction / depth * LOG2E
    first = peaks[0]
    slopes = [4.0 * LOG2E * (peaks[i] - first) for i in range(1, peaks.shape[0])]
    offsets = [
        math.log2(unit) - 2.0 * LOG2E * (peaks[i] * peaks[i] - first * first)
        for i in range(1, peaks.shape[0])
    ]

    def thickness(f):
        bumps = unit
        for k in range(len(slopes)):
            bumps = bumps + jnp.exp2(f * slopes[k] + offsets[k])
        away = f - first
        return jnp.exp2(away * away * (-2.0 * LOG2E)) * bumps

    def pack(step):
        rows = rows_of(step)

        packed = [jnp.zeros((ROWS, lanes), jnp.float32)] * groups
        for z in range(GROUP):
            here = lane_group == z
            for g in range(groups):
                v = cells[2 + g * GROUP + z, pl.ds(rows + 8, ROWS), :]
                eighth[2 + g * GROUP + z, pl.ds(rows + 8, ROWS), :] = 0.125 * v
                thick[g * GROUP + z, pl.ds(rows, ROWS), :] = thickness(v)
                two = v - pltpu.roll(v, 2, 1)
                pair[g * GROUP + z, pl.ds(rows, ROWS), :] = two
                pair_eighth[g * GROUP + z, pl.ds(rows, ROWS), :] = 0.125 * two
                packed[g] = jnp.where(here, pltpu.roll(v, (4 * z + 2) % lanes, 1), packed[g])
        for g in range(groups):
            border[g, pl.ds(rows, ROWS), :] = packed[g]
        for g in range(0, groups, 2):
            even, odd = packed[g], packed[g + 1]
            to_right[step, g // 2] = jnp.where(first_pair, even, pltpu.roll(odd, 2, 1))
            to_left[step, g // 2] = jnp.where(first_pair, pltpu.roll(odd, lanes - 2, 1), even)

    def y_copies(step):
        right = pltpu.make_async_remote_copy(
            to_right.at[step], from_left.at[step], y_send.at[0, step], y_recv.at[0, step],
            device_id={"gy": right_y}, device_id_type=MESH,
        )
        left = pltpu.make_async_remote_copy(
            to_left.at[step], from_right.at[step], y_send.at[1, step], y_recv.at[1, step],
            device_id={"gy": left_y}, device_id_type=MESH,
        )
        return right, left

    inner = pl.ds(8, xs)
    z_copies = [
        pltpu.make_async_remote_copy(
            field.at[zs - 2 : zs], cells.at[0:2, inner, :], z_send.at[0], z_recv.at[0],
            device_id={"gz": right_z}, device_id_type=MESH,
        ),
        pltpu.make_async_remote_copy(
            field.at[0:2], cells.at[zs + 2 : zs + 4, inner, :], z_send.at[1], z_recv.at[1],
            device_id={"gz": left_z}, device_id_type=MESH,
        ),
    ]
    x_right = pltpu.make_async_remote_copy(
        field.at[:, xs - 2 : xs, :], cells.at[2 : zs + 2, 6:8, :], x_send.at[0], x_recv.at[0],
        device_id={"gx": right_x}, device_id_type=MESH,
    )
    x_left = pltpu.make_async_remote_copy(
        field.at[:, 0:2, :], cells.at[2 : zs + 2, xs + 8 : xs + 10, :], x_send.at[1],
        x_recv.at[1], device_id={"gx": left_x}, device_id_type=MESH,
    )

    greet = (nz - 1 - mz) // 2 + 1

    @pl.loop(0, blocks)
    def _(step):
        load(step).wait()
        pack(step)

        @pl.when(step == greet)
        def _():
            pl.semaphore_wait(barrier, greeted)
            for copy in z_copies:
                copy.start()

            @pl.loop(0, greet)
            def _(ready):
                for copy in y_copies(ready):
                    copy.start()

            @pl.when(mx > 0)
            def _():
                pl.semaphore_signal(
                    entered.at[1], inc=1, device_id={"gx": left_x}, device_id_type=MESH
                )
                x_left.start()

            @pl.when(mx == nx - 1)
            def _():
                pl.semaphore_signal(
                    entered.at[0], inc=1, device_id={"gx": right_x}, device_id_type=MESH
                )
                x_right.start()

        @pl.when(step >= greet)
        def _():
            for copy in y_copies(step):
                copy.start()

    def corrections(step, p):
        rows = rows_of(step)
        left, right = from_left[step, p], from_right[step, p]
        fixes = []
        for odd in range(2):
            if odd:
                left, right = pltpu.roll(left, lanes - 2, 1), pltpu.roll(right, 2, 1)
            outer = jnp.where(first_pair, left, right)
            diff = outer - border[2 * p + odd, pl.ds(rows, ROWS), :]
            p2, p1 = pltpu.roll(diff, lanes - 2, 1), pltpu.roll(diff, lanes - 1, 1)
            m2, m1 = pltpu.roll(diff, 2, 1), pltpu.roll(diff, 1, 1)
            far = 0.125 * jnp.where(first_pair, -p2, m2)
            near = jnp.where(lane_column == 1, p1, jnp.where(lane_column == 2, -m1, 0.0))
            fixes.append(near + far)
        return fixes

    tints = [0.5 * tint[c] for c in range(3)]
    lights = [0.7 * light[c] for c in range(3)]
    edge = (lane < 2) | (lane >= lanes - 2)

    def march(step):
        rows = rows_of(step)
        base = rows + 8
        mid = pl.ds(base, ROWS)

        def one_pair(p, carry):
            fixes = corrections(step, p)

            def one_group(odd, carry):
                total, trans, s0, s1, s2, s3 = carry
                for zl in range(GROUP):
                    z = (2 * p + odd) * GROUP + zl + 2
                    f = cells[z, mid, :]
                    gz = (cells[z + 1, mid, :] - cells[z - 1, mid, :]) - (
                        eighth[z + 2, mid, :] - eighth[z - 2, mid, :]
                    )
                    gx = (
                        cells[z, pl.ds(base + 1, ROWS), :] - cells[z, pl.ds(base - 1, ROWS), :]
                    ) - (eighth[z, pl.ds(base + 2, ROWS), :] - eighth[z, pl.ds(base - 2, ROWS), :])
                    two8 = pair_eighth[z - 2, pl.ds(rows, ROWS), :]
                    gy = pltpu.roll(pair[z - 2, pl.ds(rows, ROWS), :], lanes - 1, 1) - (
                        pltpu.roll(two8, lanes - 2, 1) + two8
                    )
                    fix = pltpu.roll(fixes[odd], (2 * lanes - 2 - 4 * zl) % lanes, 1)
                    gy = jnp.where(edge, gy + fix, gy)
                    inverse = lax.rsqrt((gx * gx + gy * gy) + (gz * gz + 2.25))
                    lit = jnp.abs(gx * lights[0] + gy * lights[1] + gz * lights[2])
                    total = total - thick[z - 2, pl.ds(rows, ROWS), :]
                    after = jnp.exp2(total)
                    shaded = (trans - after) * (0.3 + lit * inverse)
                    trans = after
                    s0 = s0 + shaded
                    s1 = s1 + shaded * jnp.tanh(f * tints[0])
                    s2 = s2 + shaded * jnp.tanh(f * tints[1])
                    s3 = s3 + shaded * jnp.tanh(f * tints[2])
                return total, trans, s0, s1, s2, s3

            return one_group(1, one_group(0, carry))

        zero = jnp.zeros((ROWS, lanes), jnp.float32)
        start = (zero, zero + 1.0, zero, zero, zero, zero)
        total, _, s0, s1, s2, s3 = lax.fori_loop(0, groups // 2, one_pair, start)
        return 0.5 * (s0 + s1), 0.5 * (s0 + s2), 0.5 * (s0 + s3), total

    def p_copy(step):
        return pltpu.make_async_remote_copy(
            piece.at[step], pieces.at[mz], p_send.at[step], p_recv.at[mz],
            device_id={"gz": block_of(step)}, device_id_type=MESH,
        )

    for copy in z_copies:
        copy.wait_recv()
    for z in (0, 1, zs + 2, zs + 3):
        eighth[z, inner, :] = 0.125 * cells[z, inner, :]

    @pl.loop(0, blocks)
    def _(step):
        @pl.when(step == SEND_X)
        def _():
            @pl.when(mx == 0)
            def _():
                pl.semaphore_wait(entered.at[0], 1)
                x_left.start()

            @pl.when(mx < nx - 1)
            def _():
                pl.semaphore_wait(entered.at[1], 1)
                x_right.start()

        @pl.when(step == zero_step)
        def _():
            x_left.wait_recv()
            x_right.wait_recv()

            @pl.loop(0, zs // 8)
            def _(i):
                for rows in (pl.ds(6, 2), pl.ds(xs + 8, 2)):
                    z8 = pl.ds(i * 8 + 2, 8)
                    eighth[z8, rows, :] = 0.125 * cells[z8, rows, :]

        for copy in y_copies(step):
            copy.wait_recv()
        results = march(step)

        @pl.when(step < blocks - 1)
        def _():
            for c in range(4):
                piece[step, c] = results[c]
            p_copy(step).start()

        @pl.when(step == blocks - 1)
        def _():
            for c in range(4):
                pieces[mz, c] = results[c]

    for k in range(1, nz):
        source = lax.rem(mz + k, nz)
        pltpu.make_async_remote_copy(
            piece.at[0], pieces.at[source], p_send.at[0], p_recv.at[source],
            device_id={"gz": source}, device_id_type=MESH,
        ).wait_recv()

    before = None
    for k in range(nz):
        if k == 0:
            image = [pieces[0, c] for c in range(3)]
            optical = pieces[0, 3]
        else:
            before = jnp.exp2(optical)
            image = [image[c] + before * pieces[k, c] for c in range(3)]
            optical = optical + pieces[k, 3]
    for c in range(3):
        out[c] = image[c]
    out[3] = 1.0 - jnp.exp2(optical)

    for copy in (x_left, x_right, *z_copies):
        copy.wait_send()
    for step in range(blocks):
        for copy in y_copies(step):
            copy.wait_send()
    for step in range(blocks - 1):
        p_copy(step).wait_send()


def render(sizes, field, peaks, tint, light):
    nx, ny, nz = sizes
    zs, xs, lanes = field.shape
    groups, blocks = zs // GROUP, xs // ROWS
    f32 = jnp.float32
    packed = pltpu.VMEM((blocks, groups // 2, ROWS, lanes), f32)
    dma = pltpu.SemaphoreType.DMA
    smem = pl.BlockSpec(memory_space=pltpu.SMEM)
    return pl.pallas_call(
        functools.partial(kernel, nx, ny, nz, zs * nz),
        out_shape=jax.ShapeDtypeStruct((4, ROWS, lanes), f32),
        in_specs=[pl.BlockSpec(memory_space=pl.ANY), smem, smem, smem],
        out_specs=pl.BlockSpec(memory_space=pltpu.VMEM),
        scratch_shapes=[
            pltpu.VMEM((zs + 4, xs + 16, lanes), f32),
            pltpu.VMEM((zs + 4, xs + 16, lanes), f32),
            pltpu.VMEM((zs, xs, lanes), f32),
            pltpu.VMEM((zs, xs, lanes), f32),
            pltpu.VMEM((zs, xs, lanes), f32),
            pltpu.VMEM((groups, xs, lanes), f32),
            packed, packed, packed, packed,
            pltpu.VMEM((blocks, 4, ROWS, lanes), f32),
            pltpu.VMEM((nz, 4, ROWS, lanes), f32),
            dma((blocks,)), dma((2,)), dma((2,)), dma((2,)), dma((2,)),
            dma((2, blocks)), dma((2, blocks)), dma((blocks,)), dma((nz,)),
            pltpu.SemaphoreType.REGULAR((2,)),
        ],
        compiler_params=pltpu.CompilerParams(
            collective_id=0, has_side_effects=True, vmem_limit_bytes=62 << 20
        ),
    )(field, peaks, tint, light)


def solution(mesh):
    sizes = (mesh.shape["gx"], mesh.shape["gy"], mesh.shape["gz"])
    in_specs = (P("gz", "gx", "gy"), P(), P(), P())
    out_specs = P(None, ("gx", "gz"), "gy")
    return jax.shard_map(
        functools.partial(render, sizes),
        mesh=mesh, in_specs=in_specs, out_specs=out_specs, check_vma=False,
    )
```

```python
import functools
import math

import jax
import jax.numpy as jnp
from jax import lax
from jax.experimental import pallas as pl
from jax.experimental.pallas import tpu as pltpu
from jax.sharding import PartitionSpec as P

extinction = 1.5
LOG2E = math.log2(math.e)
MESH = pl.DeviceIdType.MESH
ROWS = 16
GROUP = 32
AHEAD = 3
SEND_X = 2


def kernel(
    nx, ny, nz, depth, field, peaks_in, tint_in, light_in, pieces, peaks, tint, light,
    cells, eighth, pair, pair_eighth, thick, border, to_right, to_left, from_left, from_right, piece,
    scalar_sem, load_sem, x_send, x_recv, z_send, z_recv, y_send, y_recv, p_send, p_recv, entered,
):
    zs, xs, lanes = field.shape
    groups = zs // GROUP
    blocks = xs // ROWS
    mx, my, mz = lax.axis_index("gx"), lax.axis_index("gy"), lax.axis_index("gz")
    left_x, right_x = lax.rem(mx + nx - 1, nx), lax.rem(mx + 1, nx)
    left_y, right_y = lax.rem(my + ny - 1, ny), lax.rem(my + 1, ny)
    left_z, right_z = lax.rem(mz + nz - 1, nz), lax.rem(mz + 1, nz)

    above_zero, is_last = (mz + nz - 1) // nz, (mz + 1) // nz
    zero_step = nz - 3

    def reached(step, bound):
        return (step + nz - bound) // nz

    early = above_zero * (1 - reached(mz, nz // 2))

    def block_of(step):
        at_own = reached(step, nz - 1)
        at_first = reached(step, zero_step) - reached(step, zero_step + 1)
        at_second = reached(step, nz - 2) - at_own
        place = step + 1 - above_zero * reached(step, zero_step + 1)
        inner_block = place + above_zero * reached(place, mz)
        first_block = above_zero * early * (nz - 1) + (1 - above_zero) * inner_block
        second_block = (1 - early) * (is_last * inner_block + (1 - is_last) * (nz - 1))
        return (
            at_own * mz
            + at_first * first_block
            + at_second * second_block
            + (1 - at_own - at_first - at_second) * inner_block
        )

    def rows_of(step):
        return pl.multiple_of(block_of(step) * ROWS, ROWS)

    def load(step):
        return pltpu.make_async_copy(
            field.at[:, pl.ds(rows_of(step), ROWS), :],
            cells.at[2 : zs + 2, pl.ds(rows_of(step) + 8, ROWS), :],
            load_sem.at[step],
        )

    for step in range(AHEAD):
        load(step).start()
    scalars = [
        pltpu.make_async_copy(source, target, scalar_sem.at[k])
        for k, (source, target) in enumerate(
            ((peaks_in, peaks), (tint_in, tint), (light_in, light))
        )
    ]
    for copy in scalars:
        copy.start()

    barrier = pltpu.get_barrier_semaphore()
    above_first, at_last = (mx + nx - 1) // nx, (mx + 1) // nx

    @pl.when(mx < nx - 1)
    def _():
        pl.semaphore_signal(barrier, inc=1, device_id={"gx": right_x}, device_id_type=MESH)

    @pl.when(mx == 0)
    def _():
        pl.semaphore_signal(barrier, inc=1, device_id={"gx": left_x}, device_id_type=MESH)

    for who in (left_y, right_y):
        pl.semaphore_signal(barrier, inc=1, device_id={"gy": who}, device_id_type=MESH)
    for k in range(1, nz):
        pl.semaphore_signal(
            barrier, inc=1, device_id={"gz": lax.rem(mz + k, nz)}, device_id_type=MESH
        )
    greeted = nz + 1 + above_first + at_last

    for copy in scalars:
        copy.wait()
    lane = lax.broadcasted_iota(jnp.int32, (ROWS, lanes), 1)
    lane_group = lane >> 2
    lane_column = lane & 3
    first_pair = lane_column < 2

    unit = extinction / depth * LOG2E
    first = peaks[0]
    slopes = [4.0 * LOG2E * (peaks[i] - first) for i in range(1, peaks.shape[0])]
    offsets = [
        math.log2(unit) - 2.0 * LOG2E * (peaks[i] * peaks[i] - first * first)
        for i in range(1, peaks.shape[0])
    ]

    def thickness(f):
        bumps = unit
        for k in range(len(slopes)):
            bumps = bumps + jnp.exp2(f * slopes[k] + offsets[k])
        away = f - first
        return jnp.exp2(away * away * (-2.0 * LOG2E)) * bumps

    def pack(step):
        rows = rows_of(step)

        packed = [jnp.zeros((ROWS, lanes), jnp.float32)] * groups
        for z in range(GROUP):
            here = lane_group == z
            for g in range(groups):
                v = cells[2 + g * GROUP + z, pl.ds(rows + 8, ROWS), :]
                eighth[2 + g * GROUP + z, pl.ds(rows + 8, ROWS), :] = 0.125 * v
                thick[g * GROUP + z, pl.ds(rows, ROWS), :] = thickness(v)
                two = v - pltpu.roll(v, 2, 1)
                pair[g * GROUP + z, pl.ds(rows, ROWS), :] = two
                pair_eighth[g * GROUP + z, pl.ds(rows, ROWS), :] = 0.125 * two
                packed[g] = jnp.where(here, pltpu.roll(v, (4 * z + 2) % lanes, 1), packed[g])
        for g in range(groups):
            border[g, pl.ds(rows, ROWS), :] = packed[g]
        for g in range(0, groups, 2):
            even, odd = packed[g], packed[g + 1]
            to_right[step, g // 2] = jnp.where(first_pair, even, pltpu.roll(odd, 2, 1))
            to_left[step, g // 2] = jnp.where(first_pair, pltpu.roll(odd, lanes - 2, 1), even)

    def y_copies(step):
        right = pltpu.make_async_remote_copy(
            to_right.at[step], from_left.at[step], y_send.at[0, step], y_recv.at[0, step],
            device_id={"gy": right_y}, device_id_type=MESH,
        )
        left = pltpu.make_async_remote_copy(
            to_left.at[step], from_right.at[step], y_send.at[1, step], y_recv.at[1, step],
            device_id={"gy": left_y}, device_id_type=MESH,
        )
        return right, left

    inner = pl.ds(8, xs)
    z_copies = [
        pltpu.make_async_remote_copy(
            field.at[zs - 2 : zs], cells.at[0:2, inner, :], z_send.at[0], z_recv.at[0],
            device_id={"gz": right_z}, device_id_type=MESH,
        ),
        pltpu.make_async_remote_copy(
            field.at[0:2], cells.at[zs + 2 : zs + 4, inner, :], z_send.at[1], z_recv.at[1],
            device_id={"gz": left_z}, device_id_type=MESH,
        ),
    ]
    x_right = pltpu.make_async_remote_copy(
        field.at[:, xs - 2 : xs, :], cells.at[2 : zs + 2, 6:8, :], x_send.at[0], x_recv.at[0],
        device_id={"gx": right_x}, device_id_type=MESH,
    )
    x_left = pltpu.make_async_remote_copy(
        field.at[:, 0:2, :], cells.at[2 : zs + 2, xs + 8 : xs + 10, :], x_send.at[1],
        x_recv.at[1], device_id={"gx": left_x}, device_id_type=MESH,
    )

    greet = (nz - 1 - mz) // 2 + 1

    @pl.loop(0, blocks)
    def _(step):
        load(step).wait()

        @pl.when(step + AHEAD < blocks)
        def _():
            load(step + AHEAD).start()

        pack(step)

        @pl.when(step == greet)
        def _():
            pl.semaphore_wait(barrier, greeted)
            for copy in z_copies:
                copy.start()

            @pl.loop(0, greet)
            def _(ready):
                for copy in y_copies(ready):
                    copy.start()

            @pl.when(mx > 0)
            def _():
                pl.semaphore_signal(
                    entered.at[1], inc=1, device_id={"gx": left_x}, device_id_type=MESH
                )
                x_left.start()

            @pl.when(mx == nx - 1)
            def _():
                pl.semaphore_signal(
                    entered.at[0], inc=1, device_id={"gx": right_x}, device_id_type=MESH
                )
                x_right.start()

        @pl.when(step >= greet)
        def _():
            for copy in y_copies(step):
                copy.start()

    def corrections(step, p):
        rows = rows_of(step)
        left, right = from_left[step, p], from_right[step, p]
        fixes = []
        for odd in range(2):
            if odd:
                left, right = pltpu.roll(left, lanes - 2, 1), pltpu.roll(right, 2, 1)
            outer = jnp.where(first_pair, left, right)
            diff = outer - border[2 * p + odd, pl.ds(rows, ROWS), :]
            p2, p1 = pltpu.roll(diff, lanes - 2, 1), pltpu.roll(diff, lanes - 1, 1)
            m2, m1 = pltpu.roll(diff, 2, 1), pltpu.roll(diff, 1, 1)
            far = 0.125 * jnp.where(first_pair, -p2, m2)
            near = jnp.where(lane_column == 1, p1, jnp.where(lane_column == 2, -m1, 0.0))
            fixes.append(near + far)
        return fixes

    tints = [0.5 * tint[c] for c in range(3)]
    lights = [0.7 * light[c] for c in range(3)]
    edge = (lane < 2) | (lane >= lanes - 2)

    def march(step):
        rows = rows_of(step)
        base = rows + 8
        mid = pl.ds(base, ROWS)

        def one_pair(p, carry):
            fixes = corrections(step, p)

            def one_group(odd, carry):
                total, trans, s0, s1, s2, s3 = carry
                for zl in range(GROUP):
                    z = (2 * p + odd) * GROUP + zl + 2
                    f = cells[z, mid, :]
                    gz = (cells[z + 1, mid, :] - cells[z - 1, mid, :]) - (
                        eighth[z + 2, mid, :] - eighth[z - 2, mid, :]
                    )
                    gx = (
                        cells[z, pl.ds(base + 1, ROWS), :] - cells[z, pl.ds(base - 1, ROWS), :]
                    ) - (eighth[z, pl.ds(base + 2, ROWS), :] - eighth[z, pl.ds(base - 2, ROWS), :])
                    two8 = pair_eighth[z - 2, pl.ds(rows, ROWS), :]
                    gy = pltpu.roll(pair[z - 2, pl.ds(rows, ROWS), :], lanes - 1, 1) - (
                        pltpu.roll(two8, lanes - 2, 1) + two8
                    )
                    fix = pltpu.roll(fixes[odd], (2 * lanes - 2 - 4 * zl) % lanes, 1)
                    gy = jnp.where(edge, gy + fix, gy)
                    inverse = lax.rsqrt((gx * gx + gy * gy) + (gz * gz + 2.25))
                    lit = jnp.abs(gx * lights[0] + gy * lights[1] + gz * lights[2])
                    total = total - thick[z - 2, pl.ds(rows, ROWS), :]
                    after = jnp.exp2(total)
                    shaded = (trans - after) * (0.3 + lit * inverse)
                    trans = after
                    s0 = s0 + shaded
                    s1 = s1 + shaded * jnp.tanh(f * tints[0])
                    s2 = s2 + shaded * jnp.tanh(f * tints[1])
                    s3 = s3 + shaded * jnp.tanh(f * tints[2])
                return total, trans, s0, s1, s2, s3

            return one_group(1, one_group(0, carry))

        zero = jnp.zeros((ROWS, lanes), jnp.float32)
        start = (zero, zero + 1.0, zero, zero, zero, zero)
        total, _, s0, s1, s2, s3 = lax.fori_loop(0, groups // 2, one_pair, start)
        return 0.5 * (s0 + s1), 0.5 * (s0 + s2), 0.5 * (s0 + s3), total

    def p_copy(step):
        return pltpu.make_async_remote_copy(
            piece.at[step], pieces.at[mz], p_send.at[step], p_recv.at[mz],
            device_id={"gz": block_of(step)}, device_id_type=MESH,
        )

    for copy in z_copies:
        copy.wait_recv()
    for z in (0, 1, zs + 2, zs + 3):
        eighth[z, inner, :] = 0.125 * cells[z, inner, :]

    @pl.loop(0, blocks)
    def _(step):
        @pl.when(step == SEND_X)
        def _():
            @pl.when(mx == 0)
            def _():
                pl.semaphore_wait(entered.at[0], 1)
                x_left.start()

            @pl.when(mx < nx - 1)
            def _():
                pl.semaphore_wait(entered.at[1], 1)
                x_right.start()

        @pl.when(step == zero_step)
        def _():
            x_left.wait_recv()
            x_right.wait_recv()

            @pl.loop(0, zs // 8)
            def _(i):
                for rows in (pl.ds(6, 2), pl.ds(xs + 8, 2)):
                    z8 = pl.ds(i * 8 + 2, 8)
                    eighth[z8, rows, :] = 0.125 * cells[z8, rows, :]

        for copy in y_copies(step):
            copy.wait_recv()
        results = march(step)

        for c in range(4):
            piece[step, c] = results[c]

        @pl.when(step < blocks - 1)
        def _():
            p_copy(step).start()

    own = pltpu.make_async_copy(piece.at[blocks - 1], pieces.at[mz], p_recv.at[mz])
    own.start()
    for k in range(1, nz):
        source = lax.rem(mz + k, nz)
        pltpu.make_async_remote_copy(
            piece.at[0], pieces.at[source], p_send.at[0], p_recv.at[source],
            device_id={"gz": source}, device_id_type=MESH,
        ).wait_recv()
    own.wait()

    for copy in (x_left, x_right, *z_copies):
        copy.wait_send()
    for step in range(blocks):
        for copy in y_copies(step):
            copy.wait_send()
    for step in range(blocks - 1):
        p_copy(step).wait_send()


def composite(nz, pieces, out):
    image = [pieces[0, c] for c in range(3)]
    optical = pieces[0, 3]
    for k in range(1, nz):
        before = jnp.exp2(optical)
        image = [image[c] + before * pieces[k, c] for c in range(3)]
        optical = optical + pieces[k, 3]
    for c in range(3):
        out[c] = image[c]
    out[3] = 1.0 - jnp.exp2(optical)


def render(sizes, field, peaks, tint, light):
    nx, ny, nz = sizes
    zs, xs, lanes = field.shape
    groups, blocks = zs // GROUP, xs // ROWS
    f32 = jnp.float32
    packed = pltpu.VMEM((blocks, groups // 2, ROWS, lanes), f32)
    dma = pltpu.SemaphoreType.DMA
    pieces = pl.pallas_call(
        functools.partial(kernel, nx, ny, nz, zs * nz),
        out_shape=jax.ShapeDtypeStruct((nz, 4, ROWS, lanes), f32),
        in_specs=[pl.BlockSpec(memory_space=pl.ANY)] * 4,
        out_specs=pl.BlockSpec(memory_space=pl.ANY),
        scratch_shapes=[
            *(pltpu.SMEM(a.shape, f32) for a in (peaks, tint, light)),
            pltpu.VMEM((zs + 4, xs + 16, lanes), f32),
            pltpu.VMEM((zs + 4, xs + 16, lanes), f32),
            pltpu.VMEM((zs, xs, lanes), f32),
            pltpu.VMEM((zs, xs, lanes), f32),
            pltpu.VMEM((zs, xs, lanes), f32),
            pltpu.VMEM((groups, xs, lanes), f32),
            packed, packed, packed, packed,
            pltpu.VMEM((blocks, 4, ROWS, lanes), f32),
            dma((3,)), dma((blocks,)), dma((2,)), dma((2,)), dma((2,)), dma((2,)),
            dma((2, blocks)), dma((2, blocks)), dma((blocks,)), dma((nz,)),
            pltpu.SemaphoreType.REGULAR((2,)),
        ],
        compiler_params=pltpu.CompilerParams(
            collective_id=0, has_side_effects=True, vmem_limit_bytes=62 << 20
        ),
    )(field, peaks, tint, light)
    return pl.pallas_call(
        functools.partial(composite, nz),
        out_shape=jax.ShapeDtypeStruct((4, ROWS, lanes), f32),
    )(pieces)


def solution(mesh):
    sizes = (mesh.shape["gx"], mesh.shape["gy"], mesh.shape["gz"])
    in_specs = (P("gz", "gx", "gy"), P(), P(), P())
    out_specs = P(None, ("gx", "gz"), "gy")
    return jax.shard_map(
        functools.partial(render, sizes),
        mesh=mesh, in_specs=in_specs, out_specs=out_specs, check_vma=False,
    )
```

```python
import functools
import math

import jax
import jax.numpy as jnp
from jax import lax
from jax.experimental import pallas as pl
from jax.experimental.pallas import tpu as pltpu
from jax.sharding import PartitionSpec as P

extinction = 1.5
LOG2E = math.log2(math.e)
MESH = pl.DeviceIdType.MESH
ROWS = 16
GROUP = 32
AHEAD = 3
SEND_X = 2


def kernel(
    nx, ny, nz, depth, field, peaks_in, tint_in, light_in, pieces, peaks, tint, light,
    cells, eighth, pair, pair_eighth, thick, border, to_right, to_left, from_left, from_right, piece,
    scalar_sem, load_sem, x_send, x_recv, z_send, z_recv, y_send, y_recv, p_send, p_recv, entered,
):
    zs, xs, lanes = field.shape
    groups = zs // GROUP
    blocks = xs // ROWS
    mx, my, mz = lax.axis_index("gx"), lax.axis_index("gy"), lax.axis_index("gz")
    left_x, right_x = lax.rem(mx + nx - 1, nx), lax.rem(mx + 1, nx)
    left_y, right_y = lax.rem(my + ny - 1, ny), lax.rem(my + 1, ny)
    left_z, right_z = lax.rem(mz + nz - 1, nz), lax.rem(mz + 1, nz)

    above_zero, is_last = (mz + nz - 1) // nz, (mz + 1) // nz
    zero_step = nz - 3

    def reached(step, bound):
        return (step + nz - bound) // nz

    early = above_zero * (1 - reached(mz, nz // 2))

    def block_of(step):
        at_own = reached(step, nz - 1)
        at_first = reached(step, zero_step) - reached(step, zero_step + 1)
        at_second = reached(step, nz - 2) - at_own
        place = step + 1 - above_zero * reached(step, zero_step + 1)
        inner_block = place + above_zero * reached(place, mz)
        first_block = above_zero * early * (nz - 1) + (1 - above_zero) * inner_block
        second_block = (1 - early) * (is_last * inner_block + (1 - is_last) * (nz - 1))
        return (
            at_own * mz
            + at_first * first_block
            + at_second * second_block
            + (1 - at_own - at_first - at_second) * inner_block
        )

    def rows_of(step):
        return pl.multiple_of(block_of(step) * ROWS, ROWS)

    def load(step):
        return pltpu.make_async_copy(
            field.at[:, pl.ds(rows_of(step), ROWS), :],
            cells.at[2 : zs + 2, pl.ds(rows_of(step) + 8, ROWS), :],
            load_sem.at[step],
        )

    for step in range(AHEAD):
        load(step).start()
    scalars = [
        pltpu.make_async_copy(source, target, scalar_sem.at[k])
        for k, (source, target) in enumerate(
            ((peaks_in, peaks), (tint_in, tint), (light_in, light))
        )
    ]
    for copy in scalars:
        copy.start()

    barrier = pltpu.get_barrier_semaphore()
    above_first, at_last = (mx + nx - 1) // nx, (mx + 1) // nx

    @pl.when(mx < nx - 1)
    def _():
        pl.semaphore_signal(barrier, inc=1, device_id={"gx": right_x}, device_id_type=MESH)

    @pl.when(mx == 0)
    def _():
        pl.semaphore_signal(barrier, inc=1, device_id={"gx": left_x}, device_id_type=MESH)

    for who in (left_y, right_y):
        pl.semaphore_signal(barrier, inc=1, device_id={"gy": who}, device_id_type=MESH)
    for k in range(1, nz):
        pl.semaphore_signal(
            barrier, inc=1, device_id={"gz": lax.rem(mz + k, nz)}, device_id_type=MESH
        )
    greeted = nz + 1 + above_first + at_last

    for copy in scalars:
        copy.wait()
    lane = lax.broadcasted_iota(jnp.int32, (ROWS, lanes), 1)
    lane_group = lane >> 2
    lane_column = lane & 3
    first_pair = lane_column < 2

    unit = extinction / depth * LOG2E
    first = peaks[0]
    slopes = [4.0 * LOG2E * (peaks[i] - first) for i in range(1, peaks.shape[0])]
    offsets = [
        math.log2(unit) - 2.0 * LOG2E * (peaks[i] * peaks[i] - first * first)
        for i in range(1, peaks.shape[0])
    ]

    def thickness(f):
        bumps = unit
        for k in range(len(slopes)):
            bumps = bumps + jnp.exp2(f * slopes[k] + offsets[k])
        away = f - first
        return jnp.exp2(away * away * (-2.0 * LOG2E)) * bumps

    def pack(step):
        rows = rows_of(step)

        packed = [jnp.zeros((ROWS, lanes), jnp.float32)] * groups
        for z in range(GROUP):
            here = lane_group == z
            for g in range(groups):
                v = cells[2 + g * GROUP + z, pl.ds(rows + 8, ROWS), :]
                eighth[2 + g * GROUP + z, pl.ds(rows + 8, ROWS), :] = 0.125 * v
                thick[g * GROUP + z, pl.ds(rows, ROWS), :] = thickness(v)
                two = v - pltpu.roll(v, 2, 1)
                pair[g * GROUP + z, pl.ds(rows, ROWS), :] = two
                pair_eighth[g * GROUP + z, pl.ds(rows, ROWS), :] = 0.125 * two
                packed[g] = jnp.where(here, pltpu.roll(v, (4 * z + 2) % lanes, 1), packed[g])
        for g in range(groups):
            border[g, pl.ds(rows, ROWS), :] = packed[g]
        for g in range(0, groups, 2):
            even, odd = packed[g], packed[g + 1]
            to_right[step, g // 2] = jnp.where(first_pair, even, pltpu.roll(odd, 2, 1))
            to_left[step, g // 2] = jnp.where(first_pair, pltpu.roll(odd, lanes - 2, 1), even)

    def y_copies(step):
        right = pltpu.make_async_remote_copy(
            to_right.at[step], from_left.at[step], y_send.at[0, step], y_recv.at[0, step],
            device_id={"gy": right_y}, device_id_type=MESH,
        )
        left = pltpu.make_async_remote_copy(
            to_left.at[step], from_right.at[step], y_send.at[1, step], y_recv.at[1, step],
            device_id={"gy": left_y}, device_id_type=MESH,
        )
        return right, left

    half = xs // 2
    z_copies = []
    for part in range(2):
        rows = pl.ds(part * half, half)
        inner_rows = pl.ds(8 + part * half, half)
        z_copies.append((
            pltpu.make_async_remote_copy(
                field.at[zs - 2 : zs, rows, :], cells.at[0:2, inner_rows, :],
                z_send.at[0, part], z_recv.at[0, part],
                device_id={"gz": right_z}, device_id_type=MESH,
            ),
            pltpu.make_async_remote_copy(
                field.at[0:2, rows, :], cells.at[zs + 2 : zs + 4, inner_rows, :],
                z_send.at[1, part], z_recv.at[1, part],
                device_id={"gz": left_z}, device_id_type=MESH,
            ),
        ))

    def z_arrived(part):
        inner_rows = pl.ds(8 + part * half, half)
        for copy in z_copies[part]:
            copy.wait_recv()
        for z in (0, 1, zs + 2, zs + 3):
            eighth[z, inner_rows, :] = 0.125 * cells[z, inner_rows, :]

    x_right = pltpu.make_async_remote_copy(
        field.at[:, xs - 2 : xs, :], cells.at[2 : zs + 2, 6:8, :], x_send.at[0], x_recv.at[0],
        device_id={"gx": right_x}, device_id_type=MESH,
    )
    x_left = pltpu.make_async_remote_copy(
        field.at[:, 0:2, :], cells.at[2 : zs + 2, xs + 8 : xs + 10, :], x_send.at[1],
        x_recv.at[1], device_id={"gx": left_x}, device_id_type=MESH,
    )

    greet = 4 - 2 * reached(mz, 2) - reached(mz, nz - 2)

    @pl.loop(0, blocks)
    def _(step):
        load(step).wait()

        @pl.when(step + AHEAD < blocks)
        def _():
            load(step + AHEAD).start()

        pack(step)

        @pl.when(step == greet)
        def _():
            pl.semaphore_wait(barrier, greeted)
            for copy in (*z_copies[0], *z_copies[1]):
                copy.start()

            @pl.loop(0, greet)
            def _(ready):
                for copy in y_copies(ready):
                    copy.start()

            @pl.when(mx > 0)
            def _():
                pl.semaphore_signal(
                    entered.at[1], inc=1, device_id={"gx": left_x}, device_id_type=MESH
                )
                x_left.start()

            @pl.when(mx == nx - 1)
            def _():
                pl.semaphore_signal(
                    entered.at[0], inc=1, device_id={"gx": right_x}, device_id_type=MESH
                )
                x_right.start()

        @pl.when(step >= greet)
        def _():
            for copy in y_copies(step):
                copy.start()

    def corrections(step, p):
        rows = rows_of(step)
        left, right = from_left[step, p], from_right[step, p]
        fixes = []
        for odd in range(2):
            if odd:
                left, right = pltpu.roll(left, lanes - 2, 1), pltpu.roll(right, 2, 1)
            outer = jnp.where(first_pair, left, right)
            diff = outer - border[2 * p + odd, pl.ds(rows, ROWS), :]
            p2, p1 = pltpu.roll(diff, lanes - 2, 1), pltpu.roll(diff, lanes - 1, 1)
            m2, m1 = pltpu.roll(diff, 2, 1), pltpu.roll(diff, 1, 1)
            far = 0.125 * jnp.where(first_pair, -p2, m2)
            near = jnp.where(lane_column == 1, p1, jnp.where(lane_column == 2, -m1, 0.0))
            fixes.append(near + far)
        return fixes

    tints = [0.5 * tint[c] for c in range(3)]
    lights = [0.7 * light[c] for c in range(3)]
    edge = (lane < 2) | (lane >= lanes - 2)

    def march(step):
        rows = rows_of(step)
        base = rows + 8
        mid = pl.ds(base, ROWS)

        def one_pair(p, carry):
            fixes = corrections(step, p)

            def one_group(odd, carry):
                total, trans, s0, s1, s2, s3 = carry
                for zl in range(GROUP):
                    z = (2 * p + odd) * GROUP + zl + 2
                    f = cells[z, mid, :]
                    gz = (cells[z + 1, mid, :] - cells[z - 1, mid, :]) - (
                        eighth[z + 2, mid, :] - eighth[z - 2, mid, :]
                    )
                    gx = (
                        cells[z, pl.ds(base + 1, ROWS), :] - cells[z, pl.ds(base - 1, ROWS), :]
                    ) - (eighth[z, pl.ds(base + 2, ROWS), :] - eighth[z, pl.ds(base - 2, ROWS), :])
                    two8 = pair_eighth[z - 2, pl.ds(rows, ROWS), :]
                    gy = pltpu.roll(pair[z - 2, pl.ds(rows, ROWS), :], lanes - 1, 1) - (
                        pltpu.roll(two8, lanes - 2, 1) + two8
                    )
                    fix = pltpu.roll(fixes[odd], (2 * lanes - 2 - 4 * zl) % lanes, 1)
                    gy = jnp.where(edge, gy + fix, gy)
                    inverse = lax.rsqrt((gx * gx + gy * gy) + (gz * gz + 2.25))
                    lit = jnp.abs(gx * lights[0] + gy * lights[1] + gz * lights[2])
                    total = total - thick[z - 2, pl.ds(rows, ROWS), :]
                    after = jnp.exp2(total)
                    shaded = (trans - after) * (0.3 + lit * inverse)
                    trans = after
                    s0 = s0 + shaded
                    s1 = s1 + shaded * jnp.tanh(f * tints[0])
                    s2 = s2 + shaded * jnp.tanh(f * tints[1])
                    s3 = s3 + shaded * jnp.tanh(f * tints[2])
                return total, trans, s0, s1, s2, s3

            return one_group(1, one_group(0, carry))

        zero = jnp.zeros((ROWS, lanes), jnp.float32)
        start = (zero, zero + 1.0, zero, zero, zero, zero)
        total, _, s0, s1, s2, s3 = lax.fori_loop(0, groups // 2, one_pair, start)
        return 0.5 * (s0 + s1), 0.5 * (s0 + s2), 0.5 * (s0 + s3), total

    def p_copy(step):
        return pltpu.make_async_remote_copy(
            piece.at[step], pieces.at[mz], p_send.at[step], p_recv.at[mz],
            device_id={"gz": block_of(step)}, device_id_type=MESH,
        )

    z_arrived(0)

    @pl.loop(0, blocks)
    def _(step):
        @pl.when(step == 2)
        def _():
            z_arrived(1)

        @pl.when(step == SEND_X)
        def _():
            @pl.when(mx == 0)
            def _():
                pl.semaphore_wait(entered.at[0], 1)
                x_left.start()

            @pl.when(mx < nx - 1)
            def _():
                pl.semaphore_wait(entered.at[1], 1)
                x_right.start()

        @pl.when(step == zero_step)
        def _():
            x_left.wait_recv()
            x_right.wait_recv()

            @pl.loop(0, zs // 8)
            def _(i):
                for rows in (pl.ds(6, 2), pl.ds(xs + 8, 2)):
                    z8 = pl.ds(i * 8 + 2, 8)
                    eighth[z8, rows, :] = 0.125 * cells[z8, rows, :]

        for copy in y_copies(step):
            copy.wait_recv()
        results = march(step)

        for c in range(4):
            piece[step, c] = results[c]

        @pl.when(step < blocks - 1)
        def _():
            p_copy(step).start()

    own = pltpu.make_async_copy(piece.at[blocks - 1], pieces.at[mz], p_recv.at[mz])
    own.start()
    for k in range(1, nz):
        source = lax.rem(mz + k, nz)
        pltpu.make_async_remote_copy(
            piece.at[0], pieces.at[source], p_send.at[0], p_recv.at[source],
            device_id={"gz": source}, device_id_type=MESH,
        ).wait_recv()
    own.wait()

    for copy in (x_left, x_right, *z_copies[0], *z_copies[1]):
        copy.wait_send()
    for step in range(blocks):
        for copy in y_copies(step):
            copy.wait_send()
    for step in range(blocks - 1):
        p_copy(step).wait_send()


def composite(nz, pieces, out):
    image = [pieces[0, c] for c in range(3)]
    optical = pieces[0, 3]
    for k in range(1, nz):
        before = jnp.exp2(optical)
        image = [image[c] + before * pieces[k, c] for c in range(3)]
        optical = optical + pieces[k, 3]
    for c in range(3):
        out[c] = image[c]
    out[3] = 1.0 - jnp.exp2(optical)


def render(sizes, field, peaks, tint, light):
    nx, ny, nz = sizes
    zs, xs, lanes = field.shape
    groups, blocks = zs // GROUP, xs // ROWS
    f32 = jnp.float32
    packed = pltpu.VMEM((blocks, groups // 2, ROWS, lanes), f32)
    dma = pltpu.SemaphoreType.DMA
    pieces = pl.pallas_call(
        functools.partial(kernel, nx, ny, nz, zs * nz),
        out_shape=jax.ShapeDtypeStruct((nz, 4, ROWS, lanes), f32),
        in_specs=[pl.BlockSpec(memory_space=pl.ANY)] * 4,
        out_specs=pl.BlockSpec(memory_space=pl.ANY),
        scratch_shapes=[
            *(pltpu.SMEM(a.shape, f32) for a in (peaks, tint, light)),
            pltpu.VMEM((zs + 4, xs + 16, lanes), f32),
            pltpu.VMEM((zs + 4, xs + 16, lanes), f32),
            pltpu.VMEM((zs, xs, lanes), f32),
            pltpu.VMEM((zs, xs, lanes), f32),
            pltpu.VMEM((zs, xs, lanes), f32),
            pltpu.VMEM((groups, xs, lanes), f32),
            packed, packed, packed, packed,
            pltpu.VMEM((blocks, 4, ROWS, lanes), f32),
            dma((3,)), dma((blocks,)), dma((2,)), dma((2,)), dma((2, 2)), dma((2, 2)),
            dma((2, blocks)), dma((2, blocks)), dma((blocks,)), dma((nz,)),
            pltpu.SemaphoreType.REGULAR((2,)),
        ],
        compiler_params=pltpu.CompilerParams(
            collective_id=0, has_side_effects=True, vmem_limit_bytes=62 << 20
        ),
    )(field, peaks, tint, light)
    return pl.pallas_call(
        functools.partial(composite, nz),
        out_shape=jax.ShapeDtypeStruct((4, ROWS, lanes), f32),
    )(pieces)


def solution(mesh):
    sizes = (mesh.shape["gx"], mesh.shape["gy"], mesh.shape["gz"])
    in_specs = (P("gz", "gx", "gy"), P(), P(), P())
    out_specs = P(None, ("gx", "gz"), "gy")
    return jax.shard_map(
        functools.partial(render, sizes),
        mesh=mesh, in_specs=in_specs, out_specs=out_specs, check_vma=False,
    )
```

```python
import functools
import math

import jax
import jax.numpy as jnp
from jax import lax
from jax.experimental import pallas as pl
from jax.experimental.pallas import tpu as pltpu
from jax.sharding import PartitionSpec as P

extinction = 1.5
LOG2E = math.log2(math.e)
MESH = pl.DeviceIdType.MESH
ROWS = 16
GROUP = 32
AHEAD = 3
SEND_X = 2


def kernel(
    nx, ny, nz, depth, field, peaks_in, tint_in, light_in, pieces, peaks, tint, light,
    cells, eighth, pair, pair_eighth, thick, border, to_right, to_left, from_left, from_right, piece,
    scalar_sem, load_sem, x_send, x_recv, z_send, z_recv, y_send, y_recv, p_send, p_recv, entered,
):
    zs, xs, lanes = field.shape
    groups = zs // GROUP
    blocks = xs // ROWS
    mx, my, mz = lax.axis_index("gx"), lax.axis_index("gy"), lax.axis_index("gz")
    left_x, right_x = lax.rem(mx + nx - 1, nx), lax.rem(mx + 1, nx)
    left_y, right_y = lax.rem(my + ny - 1, ny), lax.rem(my + 1, ny)
    left_z, right_z = lax.rem(mz + nz - 1, nz), lax.rem(mz + 1, nz)

    above_zero, is_last = (mz + nz - 1) // nz, (mz + 1) // nz
    zero_step = nz - 3

    def reached(step, bound):
        return (step + nz - bound) // nz

    early = above_zero * (1 - reached(mz, nz // 2))

    def block_of(step):
        at_own = reached(step, nz - 1)
        at_first = reached(step, zero_step) - reached(step, zero_step + 1)
        at_second = reached(step, nz - 2) - at_own
        place = step + 1 - above_zero * reached(step, zero_step + 1)
        inner_block = place + above_zero * reached(place, mz)
        first_block = above_zero * early * (nz - 1) + (1 - above_zero) * inner_block
        second_block = (1 - early) * (is_last * inner_block + (1 - is_last) * (nz - 1))
        return (
            at_own * mz
            + at_first * first_block
            + at_second * second_block
            + (1 - at_own - at_first - at_second) * inner_block
        )

    def rows_of(step):
        return pl.multiple_of(block_of(step) * ROWS, ROWS)

    def load(step):
        return pltpu.make_async_copy(
            field.at[:, pl.ds(rows_of(step), ROWS), :],
            cells.at[2 : zs + 2, pl.ds(rows_of(step) + 8, ROWS), :],
            load_sem.at[step],
        )

    for step in range(AHEAD):
        load(step).start()
    scalars = [
        pltpu.make_async_copy(source, target, scalar_sem.at[k])
        for k, (source, target) in enumerate(
            ((peaks_in, peaks), (tint_in, tint), (light_in, light))
        )
    ]
    for copy in scalars:
        copy.start()

    barrier = pltpu.get_barrier_semaphore()
    above_first, at_last = (mx + nx - 1) // nx, (mx + 1) // nx

    @pl.when(mx < nx - 1)
    def _():
        pl.semaphore_signal(barrier, inc=1, device_id={"gx": right_x}, device_id_type=MESH)

    @pl.when(mx == 0)
    def _():
        pl.semaphore_signal(barrier, inc=1, device_id={"gx": left_x}, device_id_type=MESH)

    for who in (left_y, right_y):
        pl.semaphore_signal(barrier, inc=1, device_id={"gy": who}, device_id_type=MESH)
    for k in range(1, nz):
        pl.semaphore_signal(
            barrier, inc=1, device_id={"gz": lax.rem(mz + k, nz)}, device_id_type=MESH
        )
    greeted = nz + 1 + above_first + at_last

    for copy in scalars:
        copy.wait()
    lane = lax.broadcasted_iota(jnp.int32, (ROWS, lanes), 1)
    lane_group = lane >> 2
    lane_column = lane & 3
    first_pair = lane_column < 2

    unit = extinction / depth * LOG2E
    first = peaks[0]
    slopes = [4.0 * LOG2E * (peaks[i] - first) for i in range(1, peaks.shape[0])]
    offsets = [
        math.log2(unit) - 2.0 * LOG2E * (peaks[i] * peaks[i] - first * first)
        for i in range(1, peaks.shape[0])
    ]

    def thickness(f):
        bumps = unit
        for k in range(len(slopes)):
            bumps = bumps + jnp.exp2(f * slopes[k] + offsets[k])
        away = f - first
        return jnp.exp2(away * away * (-2.0 * LOG2E)) * bumps

    def pack(step):
        rows = rows_of(step)

        for z in range(GROUP):
            here = lane_group == z
            for g in range(groups):
                v = cells[2 + g * GROUP + z, pl.ds(rows + 8, ROWS), :]
                eighth[2 + g * GROUP + z, pl.ds(rows + 8, ROWS), :] = 0.125 * v
                thick[g * GROUP + z, pl.ds(rows, ROWS), :] = thickness(v)
                two = v - pltpu.roll(v, 2, 1)
                pair[g * GROUP + z, pl.ds(rows, ROWS), :] = two
                pair_eighth[g * GROUP + z, pl.ds(rows, ROWS), :] = 0.125 * two
                pltpu.store(
                    border.at[g, pl.ds(rows, ROWS), :],
                    pltpu.roll(v, (4 * z + 2) % lanes, 1),
                    mask=here,
                )
        for g in range(0, groups, 2):
            even, odd = border[g, pl.ds(rows, ROWS), :], border[g + 1, pl.ds(rows, ROWS), :]
            to_right[step, g // 2] = jnp.where(first_pair, even, pltpu.roll(odd, 2, 1))
            to_left[step, g // 2] = jnp.where(first_pair, pltpu.roll(odd, lanes - 2, 1), even)

    def y_copies(step):
        right = pltpu.make_async_remote_copy(
            to_right.at[step], from_left.at[step], y_send.at[0, step], y_recv.at[0, step],
            device_id={"gy": right_y}, device_id_type=MESH,
        )
        left = pltpu.make_async_remote_copy(
            to_left.at[step], from_right.at[step], y_send.at[1, step], y_recv.at[1, step],
            device_id={"gy": left_y}, device_id_type=MESH,
        )
        return right, left

    half = xs // 2
    z_copies = []
    for part in range(2):
        rows = pl.ds(part * half, half)
        inner_rows = pl.ds(8 + part * half, half)
        z_copies.append((
            pltpu.make_async_remote_copy(
                field.at[zs - 2 : zs, rows, :], cells.at[0:2, inner_rows, :],
                z_send.at[0, part], z_recv.at[0, part],
                device_id={"gz": right_z}, device_id_type=MESH,
            ),
            pltpu.make_async_remote_copy(
                field.at[0:2, rows, :], cells.at[zs + 2 : zs + 4, inner_rows, :],
                z_send.at[1, part], z_recv.at[1, part],
                device_id={"gz": left_z}, device_id_type=MESH,
            ),
        ))

    def z_arrived(part):
        inner_rows = pl.ds(8 + part * half, half)
        for copy in z_copies[part]:
            copy.wait_recv()
        for z in (0, 1, zs + 2, zs + 3):
            eighth[z, inner_rows, :] = 0.125 * cells[z, inner_rows, :]

    x_right = pltpu.make_async_remote_copy(
        field.at[:, xs - 2 : xs, :], cells.at[2 : zs + 2, 6:8, :], x_send.at[0], x_recv.at[0],
        device_id={"gx": right_x}, device_id_type=MESH,
    )
    x_left = pltpu.make_async_remote_copy(
        field.at[:, 0:2, :], cells.at[2 : zs + 2, xs + 8 : xs + 10, :], x_send.at[1],
        x_recv.at[1], device_id={"gx": left_x}, device_id_type=MESH,
    )

    greet = 4 - 2 * reached(mz, 2) - reached(mz, nz - 2) - is_last

    @pl.loop(0, blocks)
    def _(step):
        load(step).wait()

        @pl.when(step + AHEAD < blocks)
        def _():
            load(step + AHEAD).start()

        pack(step)

        @pl.when(step == greet)
        def _():
            pl.semaphore_wait(barrier, greeted)
            for copy in (*z_copies[0], *z_copies[1]):
                copy.start()

            @pl.loop(0, greet)
            def _(ready):
                for copy in y_copies(ready):
                    copy.start()

            @pl.when(mx > 0)
            def _():
                pl.semaphore_signal(
                    entered.at[1], inc=1, device_id={"gx": left_x}, device_id_type=MESH
                )
                x_left.start()

            @pl.when(mx == nx - 1)
            def _():
                pl.semaphore_signal(
                    entered.at[0], inc=1, device_id={"gx": right_x}, device_id_type=MESH
                )
                x_right.start()

        @pl.when(step >= greet)
        def _():
            for copy in y_copies(step):
                copy.start()

    def corrections(step, p):
        rows = rows_of(step)
        left, right = from_left[step, p], from_right[step, p]
        fixes = []
        for odd in range(2):
            if odd:
                left, right = pltpu.roll(left, lanes - 2, 1), pltpu.roll(right, 2, 1)
            outer = jnp.where(first_pair, left, right)
            diff = outer - border[2 * p + odd, pl.ds(rows, ROWS), :]
            p2, p1 = pltpu.roll(diff, lanes - 2, 1), pltpu.roll(diff, lanes - 1, 1)
            m2, m1 = pltpu.roll(diff, 2, 1), pltpu.roll(diff, 1, 1)
            far = 0.125 * jnp.where(first_pair, -p2, m2)
            near = jnp.where(lane_column == 1, p1, jnp.where(lane_column == 2, -m1, 0.0))
            fixes.append(near + far)
        return fixes

    tints = [0.5 * tint[c] for c in range(3)]
    lights = [0.7 * light[c] for c in range(3)]
    edge = (lane < 2) | (lane >= lanes - 2)

    def march(step):
        rows = rows_of(step)
        base = rows + 8
        mid = pl.ds(base, ROWS)

        def one_pair(p, carry):
            fixes = corrections(step, p)

            def one_group(odd, carry):
                total, trans, s0, s1, s2, s3 = carry
                for zl in range(GROUP):
                    z = (2 * p + odd) * GROUP + zl + 2
                    f = cells[z, mid, :]
                    gz = (cells[z + 1, mid, :] - cells[z - 1, mid, :]) - (
                        eighth[z + 2, mid, :] - eighth[z - 2, mid, :]
                    )
                    gx = (
                        cells[z, pl.ds(base + 1, ROWS), :] - cells[z, pl.ds(base - 1, ROWS), :]
                    ) - (eighth[z, pl.ds(base + 2, ROWS), :] - eighth[z, pl.ds(base - 2, ROWS), :])
                    two8 = pair_eighth[z - 2, pl.ds(rows, ROWS), :]
                    gy = pltpu.roll(pair[z - 2, pl.ds(rows, ROWS), :], lanes - 1, 1) - (
                        pltpu.roll(two8, lanes - 2, 1) + two8
                    )
                    fix = pltpu.roll(fixes[odd], (2 * lanes - 2 - 4 * zl) % lanes, 1)
                    gy = jnp.where(edge, gy + fix, gy)
                    inverse = lax.rsqrt((gx * gx + gy * gy) + (gz * gz + 2.25))
                    lit = jnp.abs(gx * lights[0] + gy * lights[1] + gz * lights[2])
                    total = total - thick[z - 2, pl.ds(rows, ROWS), :]
                    after = jnp.exp2(total)
                    shaded = (trans - after) * (0.3 + lit * inverse)
                    trans = after
                    s0 = s0 + shaded
                    s1 = s1 + shaded * jnp.tanh(f * tints[0])
                    s2 = s2 + shaded * jnp.tanh(f * tints[1])
                    s3 = s3 + shaded * jnp.tanh(f * tints[2])
                return total, trans, s0, s1, s2, s3

            return one_group(1, one_group(0, carry))

        zero = jnp.zeros((ROWS, lanes), jnp.float32)
        start = (zero, zero + 1.0, zero, zero, zero, zero)
        total, _, s0, s1, s2, s3 = lax.fori_loop(0, groups // 2, one_pair, start)
        return 0.5 * (s0 + s1), 0.5 * (s0 + s2), 0.5 * (s0 + s3), total

    def p_copy(step):
        return pltpu.make_async_remote_copy(
            piece.at[step], pieces.at[mz], p_send.at[step], p_recv.at[mz],
            device_id={"gz": block_of(step)}, device_id_type=MESH,
        )

    z_arrived(0)

    @pl.loop(0, blocks)
    def _(step):
        @pl.when(step == 2)
        def _():
            z_arrived(1)

        @pl.when(step == SEND_X)
        def _():
            @pl.when(mx == 0)
            def _():
                pl.semaphore_wait(entered.at[0], 1)
                x_left.start()

            @pl.when(mx < nx - 1)
            def _():
                pl.semaphore_wait(entered.at[1], 1)
                x_right.start()

        @pl.when(step == zero_step)
        def _():
            x_left.wait_recv()
            x_right.wait_recv()

            @pl.loop(0, zs // 8)
            def _(i):
                for rows in (pl.ds(6, 2), pl.ds(xs + 8, 2)):
                    z8 = pl.ds(i * 8 + 2, 8)
                    eighth[z8, rows, :] = 0.125 * cells[z8, rows, :]

        for copy in y_copies(step):
            copy.wait_recv()
        results = march(step)

        for c in range(4):
            piece[step, c] = results[c]

        @pl.when(step < blocks - 1)
        def _():
            p_copy(step).start()

    own = pltpu.make_async_copy(piece.at[blocks - 1], pieces.at[mz], p_recv.at[mz])
    own.start()
    for k in range(1, nz):
        source = lax.rem(mz + k, nz)
        pltpu.make_async_remote_copy(
            piece.at[0], pieces.at[source], p_send.at[0], p_recv.at[source],
            device_id={"gz": source}, device_id_type=MESH,
        ).wait_recv()
    own.wait()

    for copy in (x_left, x_right, *z_copies[0], *z_copies[1]):
        copy.wait_send()
    for step in range(blocks):
        for copy in y_copies(step):
            copy.wait_send()
    for step in range(blocks - 1):
        p_copy(step).wait_send()


def composite(nz, pieces, out):
    image = [pieces[0, c] for c in range(3)]
    optical = pieces[0, 3]
    for k in range(1, nz):
        before = jnp.exp2(optical)
        image = [image[c] + before * pieces[k, c] for c in range(3)]
        optical = optical + pieces[k, 3]
    for c in range(3):
        out[c] = image[c]
    out[3] = 1.0 - jnp.exp2(optical)


def render(sizes, field, peaks, tint, light):
    nx, ny, nz = sizes
    zs, xs, lanes = field.shape
    groups, blocks = zs // GROUP, xs // ROWS
    f32 = jnp.float32
    packed = pltpu.VMEM((blocks, groups // 2, ROWS, lanes), f32)
    dma = pltpu.SemaphoreType.DMA
    pieces = pl.pallas_call(
        functools.partial(kernel, nx, ny, nz, zs * nz),
        out_shape=jax.ShapeDtypeStruct((nz, 4, ROWS, lanes), f32),
        in_specs=[pl.BlockSpec(memory_space=pl.ANY)] * 4,
        out_specs=pl.BlockSpec(memory_space=pl.ANY),
        scratch_shapes=[
            *(pltpu.SMEM(a.shape, f32) for a in (peaks, tint, light)),
            pltpu.VMEM((zs + 4, xs + 16, lanes), f32),
            pltpu.VMEM((zs + 4, xs + 16, lanes), f32),
            pltpu.VMEM((zs, xs, lanes), f32),
            pltpu.VMEM((zs, xs, lanes), f32),
            pltpu.VMEM((zs, xs, lanes), f32),
            pltpu.VMEM((groups, xs, lanes), f32),
            packed, packed, packed, packed,
            pltpu.VMEM((blocks, 4, ROWS, lanes), f32),
            dma((3,)), dma((blocks,)), dma((2,)), dma((2,)), dma((2, 2)), dma((2, 2)),
            dma((2, blocks)), dma((2, blocks)), dma((blocks,)), dma((nz,)),
            pltpu.SemaphoreType.REGULAR((2,)),
        ],
        compiler_params=pltpu.CompilerParams(
            collective_id=0, has_side_effects=True, vmem_limit_bytes=62 << 20
        ),
    )(field, peaks, tint, light)
    return pl.pallas_call(
        functools.partial(composite, nz),
        out_shape=jax.ShapeDtypeStruct((4, ROWS, lanes), f32),
    )(pieces)


def solution(mesh):
    sizes = (mesh.shape["gx"], mesh.shape["gy"], mesh.shape["gz"])
    in_specs = (P("gz", "gx", "gy"), P(), P(), P())
    out_specs = P(None, ("gx", "gz"), "gy")
    return jax.shard_map(
        functools.partial(render, sizes),
        mesh=mesh, in_specs=in_specs, out_specs=out_specs, check_vma=False,
    )
```
